32 devices in a mesh: rep: 4 (over y, x), shard: 8 (over z, core).
Axes of the slice: x: 2, y: 2, z: 4, core: 2. Of those that a mesh axis runs over, the one named last changes fastest.
Arguments:
- layer_input: bfloat16 [32, 1024, 768], P(('rep', 'shard')), may hold values from -6 to 6
- segment_ids: int32 [32, 1024], P(('rep', 'shard')), may hold values from 0 to 5, never falling along the last dimension, each value on 1 to 800 neighbouring positions
- cotangent: bfloat16 [32, 1024, 768], P(('rep', 'shard')), may hold values from -6 to 6
- w_qkv: bfloat16 [768, 2304], P('shard'), may hold values from -0.21875 to 0.21875
- bias_query: bfloat16 [768], P('shard'), may hold values from -3 to 3
- bias_value: bfloat16 [768], P('shard'), may hold values from -3 to 3
- w_out: bfloat16 [768, 768], P('shard'), may hold values from -0.875 to 0.875
- bias_out: bfloat16 [768], P('shard'), may hold values from -3 to 3
- ln1_gain: bfloat16 [768], P('shard'), may hold values from 0.25 to 1.75
- ln1_bias: bfloat16 [768], P('shard'), may hold values from -3 to 3
- w_up: bfloat16 [768, 3072], P('shard'), may hold values from -0.21875 to 0.21875
- bias_up: bfloat16 [3072], P('shard'), may hold values from -3 to 3
- w_down: bfloat16 [3072, 768], P('shard'), may hold values from -0.109375 to 0.109375
- bias_down: bfloat16 [768], P('shard'), may hold values from -3 to 3
- ln2_gain: bfloat16 [768], P('shard'), may hold values from 0.25 to 1.75
- ln2_bias: bfloat16 [768], P('shard'), may hold values from -3 to 3
Outputs:
- layer_output: bfloat16 [32, 1024, 768], P(('rep', 'shard'))
- input_grad: bfloat16 [32, 1024, 768], P(('rep', 'shard'))
- grad_w_qkv: float32 [768, 2304], P('shard')
- grad_bias_query: float32 [768], P('shard')
- grad_bias_value: float32 [768], P('shard')
- grad_w_out: float32 [768, 768], P('shard')
- grad_bias_out: float32 [768], P('shard')
- grad_ln1_gain: float32 [768], P('shard')
- grad_ln1_bias: float32 [768], P('shard')
- grad_w_up: float32 [768, 3072], P('shard')
- grad_bias_up: float32 [3072], P('shard')
- grad_w_down: float32 [3072, 768], P('shard')
- grad_bias_down: float32 [768], P('shard')
- grad_ln2_gain: float32 [768], P('shard')
- grad_ln2_bias: float32 [768], P('shard')
The draws below stay inside these ranges and needn't reach their ends.
Inputs may be any that keep to these rules, and one draw needn't show every extreme that they name: `segment_ids`: document numbers never fall along a sequence; each document holds 1 to 800 tokens of one sequence.
All inputs are finite; a program needn't handle non-finite values.
Results may differ from the reference program's by a relative error of at most 0.02.
Values may be sent and summed in bfloat16 or wider, within the bound.
No kernel may reach another device: no remote copies, remote signals or barrier semaphores. Data moves between devices by JAX's collectives and lax.ppermute only.
A program may use at most 256 MiB of HBM per device.

```python
import math
import jax
import jax.numpy as jnp
import numpy as np
from jax import lax

D = 768
HEADS = 12
HEAD_DIM = 64
FF = 3072
LEN = 1024
SEQS = 32


def steps_of(key, dims, split, least, top_value):
    factor_of, own = 1.0, jax.random.fold_in(key, 6)
    for position, blocks in split:
        steps = jnp.exp(jax.random.uniform(jax.random.fold_in(own, position), (blocks,), jnp.float32, least / len(split), top_value / len(split)))
        factor_of = factor_of * jnp.repeat(steps, dims[position] // blocks).reshape([-1 if axis == position else 1 for axis in range(len(dims))])
    return factor_of


def length_profile(amount, total, limit, lean):
    weights = [(1 << 20) // math.isqrt(rank ** lean) + 1 for rank in range(2, amount + 1)]
    spare, given = total - limit - (amount - 1), [1] * (amount - 1)
    while spare > 0:
        candidates = [i for i in range(amount - 1) if given[i] < limit]
        whole, remaining = sum([weights[i] for i in candidates]), spare
        for i in candidates:
            more = min(limit - given[i], max(1, remaining * weights[i] // whole), spare)
            given[i] = given[i] + more
            spare = spare - more
    return np.array([limit] + given)


def ragged_sizes(key, count, total, reach, skew):
    if count == 2:
        one = jax.random.randint(key, (), max(1, total - reach), min(reach, total - 1) + 1)
        return jnp.stack([one, total - one])
    lengths = jnp.asarray(length_profile(count, total, reach, skew), jnp.int32)
    pairs = (count - 1) // 2
    giver, sink = lengths[1:1 + 2 * pairs:2], lengths[2:2 + 2 * pairs:2]
    slack = jnp.minimum(giver - 1, reach - sink)
    moved = jax.random.randint(jax.random.fold_in(key, 1), (pairs,), 0, 1 << 20) % (slack + 1)
    lengths = lengths.at[1:1 + 2 * pairs:2].set(giver - moved).at[2:2 + 2 * pairs:2].set(sink + moved)
    return lengths[jax.random.permutation(jax.random.fold_in(key, 2), count)]


def scatter_about(stream_key, dims, deviation, most, cuts=(), dtype=jnp.bfloat16):
    array = jax.random.normal(stream_key, dims, jnp.float32) * deviation
    if len(cuts) > 0:
        array = steps_of(stream_key, dims, cuts, -0.22, 0.18) * array
    return jnp.clip(array, min=-most, max=most).astype(dtype)


def setup_inputs(seed: int = 0) -> dict:
    streams_of = jax.random.split(jax.random.key(seed), 17)
    return {
        "layer_input": scatter_about(streams_of[0], (SEQS, LEN, D), 1.0, 6.0, ((0, 32),)),
        "segment_ids": jax.vmap(lambda own: jnp.searchsorted(jnp.cumsum(ragged_sizes(own, LEN // 256 + 2, LEN, LEN * 25 // 32, 0)), jnp.arange(LEN), side="right"))(jax.random.split(streams_of[1], SEQS)).reshape((SEQS, LEN)).astype(jnp.int32),
        "cotangent": scatter_about(streams_of[2], (SEQS, LEN, D), 1.0, 6.0, ((0, 32),)),
        "w_qkv": scatter_about(streams_of[3], (D, 3 * D), D ** -0.5, 0.21875, ((0, 8),)),
        "bias_query": scatter_about(streams_of[4], (D,), 0.5, 3.0, ((0, 8),)),
        "bias_value": scatter_about(streams_of[5], (D,), 0.5, 3.0, ((0, 8),)),
        "w_out": scatter_about(streams_of[6], (D, D), (D // 16) ** -0.5, 0.875, ((0, 8),)),
        "bias_out": scatter_about(streams_of[7], (D,), 0.5, 3.0, ((0, 8),)),
        "ln1_gain": jnp.clip(1.0 + 0.15 * jax.random.normal(streams_of[8], (D,), jnp.float32), 0.25, 1.75).astype(jnp.bfloat16),
        "ln1_bias": scatter_about(streams_of[9], (D,), 0.5, 3.0, ((0, 8),)),
        "w_up": scatter_about(streams_of[10], (D, FF), D ** -0.5, 0.21875, ((0, 8),)),
        "bias_up": scatter_about(streams_of[11], (FF,), 0.5, 3.0, ((0, 8),)),
        "w_down": scatter_about(streams_of[12], (FF, D), FF ** -0.5, 0.109375, ((0, 8),)),
        "bias_down": scatter_about(streams_of[13], (D,), 0.5, 3.0, ((0, 8),)),
        "ln2_gain": jnp.clip(1.0 + 0.15 * jax.random.normal(streams_of[14], (D,), jnp.float32), 0.25, 1.75).astype(jnp.bfloat16),
        "ln2_bias": scatter_about(streams_of[15], (D,), 0.5, 3.0, ((0, 8),)),
    }


highest_mode = lax.Precision.HIGHEST

@jax.custom_vjp
def low(v):
    return lax.optimization_barrier(v.astype(jnp.bfloat16)).astype(jnp.float32)

@jax.custom_vjp
def low_back(v):
    return v

def low_keep(v):
    return (low(v), None)

def low_pass(kept, grad):
    return (grad,)

def back_keep(v):
    return (v, None)

def back_low(kept, grad):
    return (low(grad),)
low.defvjp(low_keep, low_pass)
low_back.defvjp(back_keep, back_low)

def layer_norm(values, gain, shift):
    centred = values - lax.optimization_barrier(jnp.mean(values, -1, keepdims=True))
    variance = lax.optimization_barrier(jnp.mean(centred * centred, -1, keepdims=True))
    return centred * lax.rsqrt(variance + 1e-12) * gain + shift

def gelu_exact(values):
    return 0.5 * values * (1.0 + lax.erf(values * (1.0 / math.sqrt(2.0))))

def layer_one(params, tokens_seq, segment_seq):
    w_qkv, bias_query, bias_value, w_out, bias_out, ln1_gain, ln1_bias, w_up, bias_up, w_down, bias_down, ln2_gain, ln2_bias = params
    zeros_key = jnp.zeros_like(bias_query)
    projected = jnp.dot(tokens_seq, w_qkv, precision=highest_mode) + jnp.concatenate([bias_query, zeros_key, bias_value])
    projected = low(low_back(projected))
    heads_all = projected.reshape(LEN, 3, HEADS, HEAD_DIM)
    scores = jnp.einsum('qhd,khd->hqk', heads_all[:, 0], heads_all[:, 1], precision=highest_mode) * 0.125
    scores = low_back(scores)
    same_doc = segment_seq[:, None] == segment_seq[None, :]
    scores = jnp.where(same_doc[None], scores, -1e+30)
    top_score = lax.optimization_barrier(jnp.max(scores, -1, keepdims=True))
    expo = jnp.exp(scores - top_score)
    weights = low(expo / lax.optimization_barrier(jnp.sum(expo, -1, keepdims=True)))
    mixed = jnp.einsum('hqk,khd->qhd', weights, heads_all[:, 2], precision=highest_mode).reshape(LEN, D)
    mixed = low(low_back(mixed))
    hidden = tokens_seq + low_back(jnp.dot(mixed, w_out, precision=highest_mode) + bias_out)
    normed_one = low(layer_norm(hidden, ln1_gain, ln1_bias))
    inner = low_back(jnp.dot(normed_one, w_up, precision=highest_mode) + bias_up)
    activated = low(gelu_exact(inner))
    summed = normed_one + low_back(jnp.dot(activated, w_down, precision=highest_mode) + bias_down)
    return layer_norm(summed, ln2_gain, ln2_bias)

def reference(layer_input, segment_ids, cotangent, w_qkv, bias_query, bias_value, w_out, bias_out, ln1_gain, ln1_bias, w_up, bias_up, w_down, bias_down, ln2_gain, ln2_bias):
    params = tuple((weight_arg.astype(jnp.float32) for weight_arg in (w_qkv, bias_query, bias_value, w_out, bias_out, ln1_gain, ln1_bias, w_up, bias_up, w_down, bias_down, ln2_gain, ln2_bias)))
    checked_layer = jax.checkpoint(layer_one)

    def forward(tokens, weights_all):
        return lax.map(lambda seq_pair: checked_layer(weights_all, seq_pair[0], seq_pair[1]), (tokens, segment_ids))
    output, pull_back = jax.vjp(forward, layer_input.astype(jnp.float32), params)
    input_grad, grads = pull_back(cotangent.astype(jnp.float32))
    return (output.astype(jnp.bfloat16), input_grad.astype(jnp.bfloat16), grads[0], grads[1], grads[2], grads[3], grads[4], grads[5], grads[6], grads[7], grads[8], grads[9], grads[10], grads[11], grads[12])
```

```python
import functools
import math

import jax
import jax.numpy as jnp
from jax import lax
from jax.experimental import pallas as pl
from jax.experimental.pallas import tpu as pltpu
from jax.sharding import PartitionSpec as P

HEAD_DIM = 64
BIG = 2.0**100
BF = jnp.bfloat16
F32 = jnp.float32
NN = (((1,), (0,)), ((), ()))
NT = (((1,), (1,)), ((), ()))
TN = (((0,), (0,)), ((), ()))


def dot(a, b, dims=NN):
    return lax.dot_general(a, b, dims, preferred_element_type=F32)


def tree(op, x):
    while x.shape[0] > 8:
        half = x.shape[0] // 2
        x = op(x[:half], x[half:])
    return x


def split3(x):
    hi = x.astype(BF).astype(F32)
    rest = x - hi
    mid = rest.astype(BF).astype(F32)
    return hi, mid, rest - mid


def doc_features(seg):
    lane = lax.broadcasted_iota(jnp.int32, (seg.shape[0], 128), 1) % 64
    same = seg[:, None] == lane
    query_side = jnp.where(same, 1.0, 0.0).astype(BF)
    key_side = jnp.where(
        lane < 8, jnp.where(same, 0.0, -BIG), jnp.where(lane < 11, 1.0, 0.0)
    ).astype(BF)
    return query_side, key_side


def fwd_kernel(q_ref, k_ref, v_ref, fq_ref, fk_ref, o_ref, fl_ref, kh_s, vt_s, *, bq):
    length = q_ref.shape[0]
    lane = lax.broadcasted_iota(jnp.int32, (length, 128), 1)
    first = lane < 64
    k2 = k_ref[...]
    fk = fk_ref[...]
    kh_s[0] = jnp.where(first, k2, fk)
    kh_s[1] = jnp.where(first, fk, k2)
    vt_s[...] = v_ref[...].T
    firstq = lax.broadcasted_iota(jnp.int32, (bq, 128), 1) < 64
    row = lax.broadcasted_iota(jnp.int32, (128, bq), 0)
    def step(i, carry):
        rows = pl.ds(pl.multiple_of(i * bq, bq), bq)
        q2 = q_ref[rows, :] * BF(0.125)
        fq = fq_ref[rows, :]
        outs, feats = [], []
        for h in range(2):
            qh = jnp.where(firstq, q2, fq) if h == 0 else jnp.where(firstq, fq, q2)
            st = dot(kh_s[h], qh, NT)
            top = jnp.max(tree(jnp.maximum, st), 0, keepdims=True)
            ex = jnp.exp(st - top)
            tot = jnp.sum(tree(jnp.add, ex), 0, keepdims=True)
            ot = dot(vt_s[64 * h:64 * h + 64, :], ex.astype(BF))
            outs.append(ot * (1.0 / tot))
            feats.append(split3(-(top + jnp.log(tot))))
        o_ref[rows, :] = jnp.concatenate(outs, 0).T.astype(BF)
        f = jnp.zeros((128, bq), F32)
        for h in range(2):
            base = 72 if h == 0 else 8
            for j in range(3):
                f = jnp.where(row == base + j, feats[h][j], f)
        fl_ref[rows, :] = f.T.astype(BF) + fq
        return carry
    lax.fori_loop(0, length // bq, step, 0)

def attn_fwd(projected, fq, fk, bq=512):
    length = projected.shape[0]
    width = projected.shape[1] // 3
    nb = width // 128
    blk = lambda off: pl.BlockSpec((length, 128), lambda p: (0, off + p))
    full = pl.BlockSpec((length, 128), lambda p: (0, 0))
    return pl.pallas_call(
        functools.partial(fwd_kernel, bq=bq),
        grid=(nb,),
        in_specs=[blk(0), blk(nb), blk(2 * nb), full, full],
        out_specs=[blk(0), blk(0)],
        out_shape=[jax.ShapeDtypeStruct((length, width), BF)] * 2,
        scratch_shapes=[pltpu.VMEM((2, length, 128), BF), pltpu.VMEM((128, length), BF)],
        compiler_params=pltpu.CompilerParams(vmem_limit_bytes=48 << 20),
        cost_estimate=pl.CostEstimate(flops=4 * nb * 256 * length * length, bytes_accessed=10 * length * width, transcendentals=2 * nb * length * length),
        name="attn_fwd",
    )(projected, projected, projected, fq, fk)

def bwd_kernel(q_ref, k_ref, v_ref, g_ref, o_ref, fl_ref, fk_ref, dq_ref, dk_ref, dv_ref,
               qh_s, gh_s, qs_s, dqt_s, *, bk):
    length = q_ref.shape[0]
    lane = lax.broadcasted_iota(jnp.int32, (length, 128), 1)
    first = lane < 64
    q2 = q_ref[...] * BF(0.125)
    fl = fl_ref[...]
    g2 = g_ref[...]
    qs_s[...] = q2
    qh_s[0] = jnp.where(first, q2, fl)
    qh_s[1] = jnp.where(first, fl, q2)
    prod = g2.astype(F32) * o_ref[...].astype(F32)
    hi = prod.astype(BF)
    lo = (prod - hi.astype(F32)).astype(BF)
    ri = lax.broadcasted_iota(jnp.int32, (128, 128), 0)
    ci = lax.broadcasted_iota(jnp.int32, (128, 128), 1)
    cross = jnp.where((ri < 64) != (ci < 64), -1.0, 0.0).astype(BF)
    neg = dot(hi, cross) + dot(lo, cross)
    a, b, c = split3(neg)
    l64 = lane % 64
    fd = jnp.where(l64 == 8, a, jnp.where(l64 == 9, b, jnp.where(l64 == 10, c, 0.0))).astype(BF)
    gh_s[0] = jnp.where(first, g2, fd)
    gh_s[1] = jnp.where(first, fd, g2)
    dqt_s[...] = jnp.zeros_like(dqt_s)
    firstk = lax.broadcasted_iota(jnp.int32, (bk, 128), 1) < 64
    def step(i, carry):
        rows = pl.ds(pl.multiple_of(i * bk, bk), bk)
        k2 = k_ref[rows, :]
        v2 = v_ref[rows, :]
        fk = fk_ref[rows, :]
        kt = k2.T
        dks, dvs = [], []
        for h in range(2):
            kh = jnp.where(firstk, k2, fk) if h == 0 else jnp.where(firstk, fk, k2)
            vh = jnp.where(firstk, v2, fk) if h == 0 else jnp.where(firstk, fk, v2)
            pt = jnp.exp(dot(kh, qh_s[h], NT))
            dpt = dot(vh, gh_s[h], NT)
            ds = (pt * dpt).astype(BF)
            dvs.append(dot(pt.astype(BF), g_ref[...]))
            dks.append(dot(ds, qs_s[...]))
            dqt_s[64 * h:64 * h + 64, :] += dot(kt[64 * h:64 * h + 64, :], ds)
        dk_ref[rows, :] = jnp.where(firstk, dks[0], dks[1]).astype(BF)
        dv_ref[rows, :] = jnp.where(firstk, dvs[0], dvs[1]).astype(BF)
        return carry
    lax.fori_loop(0, length // bk, step, 0)
    dq_ref[...] = (dqt_s[...] * 0.125).T.astype(BF)

def attn_bwd(projected, grad_mixed, mixed, fl, fk, bk=512, first_pair=0, pairs=None):
    length = projected.shape[0]
    width = projected.shape[1] // 3
    nb = width // 128
    pairs = nb if pairs is None else pairs
    blk = lambda off: pl.BlockSpec((length, 128), lambda p: (0, off + p))
    full = pl.BlockSpec((length, 128), lambda p: (0, 0))
    f = first_pair
    return pl.pallas_call(
        functools.partial(bwd_kernel, bk=bk),
        grid=(pairs,),
        in_specs=[blk(f), blk(nb + f), blk(2 * nb + f), blk(f), blk(f), blk(f), full],
        out_specs=[blk(0), blk(0), blk(0)],
        out_shape=[jax.ShapeDtypeStruct((length, pairs * 128), BF)] * 3,
        scratch_shapes=[pltpu.VMEM((2, length, 128), BF), pltpu.VMEM((2, length, 128), BF),
                        pltpu.VMEM((length, 128), BF), pltpu.VMEM((128, length), F32)],
        compiler_params=pltpu.CompilerParams(vmem_limit_bytes=48 << 20),
        cost_estimate=pl.CostEstimate(flops=10 * pairs * 256 * length * length, bytes_accessed=18 * length * pairs * 128, transcendentals=2 * pairs * length * length),
        name="attn_bwd",
    )(projected, projected, projected, grad_mixed, mixed, fl, fk)


def layer_norm(values, gain, shift):
    centred = values - jnp.mean(values, -1, keepdims=True)
    inv_std = lax.rsqrt(jnp.mean(centred * centred, -1, keepdims=True) + 1e-12)
    normed = centred * inv_std
    return normed * gain + shift, normed, inv_std


def norm_back(grad_out, normed, inv_std, gain):
    scaled = grad_out * gain
    grad_in = inv_std * (
        scaled
        - jnp.mean(scaled, -1, keepdims=True)
        - normed * jnp.mean(scaled * normed, -1, keepdims=True)
    )
    return grad_in, jnp.sum(grad_out * normed, 0), jnp.sum(grad_out, 0)


def gelu_parts(values):
    cdf = 0.5 * (1.0 + lax.erf(values * (1.0 / math.sqrt(2.0))))
    bell = jnp.exp(-0.5 * values * values) * (1.0 / math.sqrt(2.0 * math.pi))
    return values * cdf, cdf + values * bell


def gather(x):
    return lax.all_gather(x, "shard", axis=0, tiled=True)


def rep_sum(x, reps):
    step = 1
    while step < reps:
        other = lax.ppermute(x.astype(BF), "rep", [(i, i ^ step) for i in range(reps)])
        x = x.astype(BF).astype(F32) + other.astype(F32)
        step *= 2
    return x


def body(
    shards,
    reps,
    layer_input,
    segment_ids,
    cotangent,
    w_qkv,
    bias_query,
    bias_value,
    w_out,
    bias_out,
    ln1_gain,
    ln1_bias,
    w_up,
    bias_up,
    w_down,
    bias_down,
    ln2_gain,
    ln2_bias,
):
    _, length, width = layer_input.shape
    part = width // shards
    x = layer_input.reshape(length, width)
    dy = cotangent.reshape(length, width).astype(F32)
    small = jnp.concatenate(
        [bias_query, bias_value, bias_out, ln1_gain, ln1_bias, bias_down, ln2_gain, ln2_bias, bias_up]
    )[None]
    full_qkv = gather(w_qkv)
    full_small = gather(small)
    full_out = gather(w_out)
    full_up = gather(w_up)
    full_down = gather(w_down)
    vec = lambda i: full_small[:, i * part : (i + 1) * part].reshape(-1).astype(F32)
    b_query, b_value, b_out, g_one, s_one, b_down, g_two, s_two = [vec(i) for i in range(8)]
    b_up = full_small[:, 8 * part :].reshape(-1).astype(F32)
    seg = segment_ids.reshape(length)
    feat_query, feat_key = doc_features(seg)

    qkv_bias = jnp.concatenate([b_query, jnp.zeros_like(b_query), b_value])
    projected = (dot(x, full_qkv) + qkv_bias).astype(BF)
    mixed, feat_row = attn_fwd(projected, feat_query, feat_key)
    hidden = x.astype(F32) + dot(mixed, full_out) + b_out
    normed_value, normed_one, inv_one = layer_norm(hidden, g_one, s_one)
    normed_low = normed_value.astype(BF)
    inner = dot(normed_low, full_up) + b_up
    act, slope = gelu_parts(inner)
    act = act.astype(BF)
    summed = normed_low.astype(F32) + dot(act, full_down) + b_down
    out_value, normed_two, inv_two = layer_norm(summed, g_two, s_two)
    layer_output = out_value.astype(BF).reshape(1, length, width)

    d_summed, grad_g_two, grad_s_two = norm_back(dy, normed_two, inv_two, g_two)
    d_ffn = d_summed.astype(BF)
    grad_down = dot(act, d_ffn, TN).astype(BF)
    grad_b_down = jnp.sum(d_ffn.astype(F32), 0)
    d_inner = (dot(d_ffn, full_down, NT) * slope).astype(BF)
    grad_up = dot(normed_low, d_inner, TN).astype(BF)
    grad_b_up = jnp.sum(d_inner.astype(F32), 0)
    d_normed = d_summed + dot(d_inner, full_up, NT)
    d_hidden, grad_g_one, grad_s_one = norm_back(d_normed, normed_one, inv_one, g_one)
    d_attn = d_hidden.astype(BF)
    grad_out = dot(mixed, d_attn, TN).astype(BF)
    grad_b_out = jnp.sum(d_attn.astype(F32), 0)
    d_mixed = dot(d_attn, full_out, NT).astype(BF)

    d_mixed, grad_down, grad_up, grad_out = lax.optimization_barrier(
        (d_mixed, grad_down, grad_up, grad_out)
    )
    scatter = lambda g: lax.psum_scatter(g, "shard", scatter_dimension=0, tiled=True)
    own_down = scatter(grad_down)
    own_up = scatter(grad_up)
    own_out = scatter(grad_out)
    d_query, d_key, d_value = attn_bwd(projected, d_mixed, mixed, feat_row, feat_key)
    d_projected = jnp.concatenate([d_query, d_key, d_value], -1)
    grad_qkv = dot(x, d_projected, TN).astype(BF)
    grad_b_query = jnp.sum(d_query.astype(F32), 0)
    grad_b_value = jnp.sum(d_value.astype(F32), 0)
    input_grad = (d_hidden + dot(d_projected, full_qkv, NT)).astype(BF).reshape(1, length, width)

    small_grads = jnp.concatenate(
        [
            g.reshape(shards, -1)
            for g in (
                grad_b_query,
                grad_b_value,
                grad_b_out,
                grad_g_one,
                grad_s_one,
                grad_b_down,
                grad_g_two,
                grad_s_two,
                grad_b_up,
            )
        ],
        1,
    )
    count = small_grads.shape[1]
    columns = 3 * width
    rows = -(-count // (8 * columns)) * 8
    small_rows = jnp.pad(small_grads, ((0, 0), (0, rows * columns - count))).reshape(shards, rows, columns)
    packed = jnp.concatenate([grad_qkv.reshape(shards, part, columns), small_rows.astype(BF)], 1)
    own_packed = scatter(packed.reshape(shards * (part + rows), columns))

    own_down = rep_sum(own_down, reps)
    own_up = rep_sum(own_up, reps)
    own_out = rep_sum(own_out, reps)
    own_packed = rep_sum(own_packed, reps)
    own_qkv = own_packed[:part]
    own_small = own_packed[part:].reshape(-1)
    piece = lambda i: own_small[i * part : (i + 1) * part]
    return (
        layer_output,
        input_grad,
        own_qkv,
        piece(0),
        piece(1),
        own_out,
        piece(2),
        piece(3),
        piece(4),
        own_up,
        own_small[8 * part : count],
        own_down,
        piece(5),
        piece(6),
        piece(7),
    )


def solution(mesh):
    shards, reps = mesh.shape["shard"], mesh.shape["rep"]
    rows = P(("rep", "shard"), None, None)
    mat, vec = P("shard", None), P("shard")
    return jax.shard_map(
        functools.partial(body, shards, reps),
        mesh=mesh,
        in_specs=(
            rows,
            P(("rep", "shard"), None),
            rows,
            mat,
            vec,
            vec,
            mat,
            vec,
            vec,
            vec,
            mat,
            vec,
            mat,
            vec,
            vec,
            vec,
        ),
        out_specs=(rows, rows, mat, vec, vec, mat, vec, vec, vec, mat, vec, mat, vec, vec, vec),
        check_vma=False,
    )
```
